768 devices in a mesh: energy: 96 (over x, z, y_hi), atom: 8 (over y_lo, core).
Axes of the slice: x: 4, y: 8 (y_hi: 2, y_lo: 4; y = y_hi * 4 + y_lo), z: 12, core: 2. Of those that a mesh axis runs over, the one named last changes fastest.
Arguments:
- greens: bfloat16 [2, 768, 128, 256], P(None, ('energy', 'atom')), may hold values from -6 to 6
- coupling: bfloat16 [128, 8, 256], P('atom'), may hold values from -1.5 to 1.5
- neighbours: int32 [128, 8], P('atom'), may hold values from 0 to 127, as said below
- counts: int32 [128], P('atom'), may hold values from 4 to 8, as said below
- phonon_weights: float32 [2, 16], replicated, may hold values from 0.02 to 0.12
- offsets: int32 [16], replicated, may hold values from 1 to 8, as said below
Outputs:
- self_energy: bfloat16 [2, 768, 128, 256], P(None, 'energy', 'atom')
- phonon_self: float32 [128, 128], P('atom')
- current: float32 [768, 256], P(('energy', 'atom'))
The draws below stay inside these ranges and needn't reach their ends.
Inputs may be any that keep to these rules, and one draw needn't show every extreme that they name: `neighbours`: every entry of row a differs from a by 1 to 8; in every draw some entry lies exactly 8 from its atom. Atom a uses its first counts[a] listed neighbours; every draw holds an atom with 8 and one with 4. `offsets`: every draw holds a shift of 1 and a shift of 8.
All inputs are finite; a program needn't handle non-finite values.
Results may differ from the reference program's by a relative error of at most 0.0067.
Values may be sent and summed in bfloat16 or wider, within the bound.
No kernel may reach another device: no remote copies, remote signals or barrier semaphores. Data moves between devices by JAX's collectives and lax.ppermute only.
A program may use at most 32 MiB of HBM per device.

```python
import math
import jax
import jax.numpy as jnp
from jax import lax

NO = 16
NB = 8
NW = 16
REACH = 8
NE = 768
NA = 128


def draw_neighbours(key, part):
    subkeys = jax.random.split(jax.random.fold_in(key, 11), 3)
    atom_ids = jnp.arange(NA, dtype=jnp.int32)[:, None]
    slot_ids = jnp.arange(NB, dtype=jnp.int32)[None, :]
    magnitude = jax.random.randint(subkeys[0], (NA, NB), 1, REACH + 1, dtype=jnp.int32)
    direction = jax.random.randint(subkeys[1], (NA, NB), 0, 2, dtype=jnp.int32) * 2 - 1
    chosen = jax.random.randint(subkeys[2], (), 0, NA, dtype=jnp.int32)
    magnitude = jnp.where((atom_ids == chosen) & (slot_ids == 0), REACH, magnitude)
    step_size = direction * magnitude
    target = atom_ids + step_size
    outside = (target < 0) | (target >= NA)
    return jnp.where(outside, atom_ids - step_size, target).astype(jnp.int32)


def draw_counts(key, part):
    subkeys = jax.random.split(jax.random.fold_in(key, 23), 3)
    atom_ids = jnp.arange(NA, dtype=jnp.int32)
    values = jax.random.randint(subkeys[0], (NA,), NB // 2, NB + 1, dtype=jnp.int32)
    first_pick = jax.random.randint(subkeys[1], (), 0, NA, dtype=jnp.int32)
    second_pick = (first_pick + 1 + jax.random.randint(subkeys[2], (), 0, NA - 1, dtype=jnp.int32)) % NA
    values = jnp.where(atom_ids == first_pick, NB, values)
    values = jnp.where(atom_ids == second_pick, NB // 2, values)
    return values.astype(jnp.int32)


def draw_offsets(key, part):
    subkeys = jax.random.split(jax.random.fold_in(key, 37), 3)
    freq_ids = jnp.arange(NW, dtype=jnp.int32)
    values = jax.random.randint(subkeys[0], (NW,), 1, REACH + 1, dtype=jnp.int32)
    first_pick = jax.random.randint(subkeys[1], (), 0, NW, dtype=jnp.int32)
    second_pick = (first_pick + 1 + jax.random.randint(subkeys[2], (), 0, NW - 1, dtype=jnp.int32)) % NW
    values = jnp.where(freq_ids == first_pick, REACH, values)
    values = jnp.where(freq_ids == second_pick, 1, values)
    return values.astype(jnp.int32)


def block_levels(key, dims, cuts, least, largest):
    loudness = 1.0
    for position, blocks in cuts:
        heights = jax.random.uniform(jax.random.fold_in(jax.random.fold_in(key, 6), position), (blocks,), jnp.float32, least / len(cuts), largest / len(cuts))
        loudness = loudness * jnp.repeat(jnp.exp(heights), dims[position] // blocks).reshape((-1,) + (1,) * (len(dims) - 1 - position))
    return loudness


def centred(own_key, dims, deviation, most, pieces=(), held_as=jnp.bfloat16):
    result = deviation * jax.random.normal(own_key, dims, jnp.float32)
    if pieces:
        result = result * block_levels(own_key, dims, pieces, -0.22, 0.18)
    return jnp.clip(result, -most, most).astype(held_as)


def setup_inputs(seed: int = 0) -> dict:
    keys = jax.random.split(jax.random.key(seed), 7)
    greens = centred(keys[0], (2, NE, NA, NO * NO), 1.0, 6.0, ((1, 768),))
    coupling = centred(keys[1], (NA, NB, NO * NO), NO ** -0.5, 1.5, ((0, 8),))
    neighbours = draw_neighbours(jax.random.fold_in(keys[6], 71), 0)
    counts = draw_counts(jax.random.fold_in(keys[6], 71), 0)
    phonon_weights = jnp.clip(jnp.exp(jax.random.uniform(keys[4], (2, NW), jnp.float32, math.log(0.02), math.log(0.12))), 0.02, 0.12)
    offsets = draw_offsets(jax.random.fold_in(keys[6], 71), 0)
    return dict(greens=greens, coupling=coupling, neighbours=neighbours, counts=counts, phonon_weights=phonon_weights, offsets=offsets)


def coefficients(phonon_weights, offsets):
    distance = jnp.arange(-REACH, REACH + 1, dtype=jnp.int32)[:, None]
    upward = (distance == offsets[None, :]).astype(jnp.float32)
    downward = (distance == -offsets[None, :]).astype(jnp.float32)
    emission = phonon_weights[0][None, :]
    absorption = phonon_weights[1][None, :]
    coef_less = lax.optimization_barrier(jnp.sum(emission * upward + absorption * downward, axis=1))
    coef_greater = lax.optimization_barrier(jnp.sum(emission * downward + absorption * upward, axis=1))
    return (coef_less.astype(jnp.bfloat16), coef_greater.astype(jnp.bfloat16))

def shift_mix(coef, field):
    padded = jnp.pad(field, ((REACH, REACH), (0, 0), (0, 0)))
    total = jnp.zeros(field.shape, jnp.float32)
    for offset in range(2 * REACH + 1):
        total = total + coef[offset].astype(jnp.float32) * padded[offset:offset + NE].astype(jnp.float32)
    return total.astype(jnp.bfloat16)

def reference(greens, coupling, neighbours, counts, phonon_weights, offsets):
    coef_less, coef_greater = coefficients(phonon_weights, offsets)
    mixed_less = shift_mix(coef_less, greens[0])
    mixed_greater = shift_mix(coef_greater, greens[1])
    padded_less = jnp.pad(greens[0], ((REACH, REACH), (0, 0), (0, 0)))
    scale_phonon = 1.0 / math.sqrt(NO * NO * NE)

    def slot_step(collected, slot_number):
        target = neighbours[:, slot_number]
        active = (slot_number < counts).astype(jnp.float32)
        matrix = coupling[:, slot_number].reshape(NA, NO, NO).astype(jnp.float32)
        gathered = jnp.stack([mixed_less[:, target], mixed_greater[:, target], greens[1][:, target]])
        gathered = gathered.reshape(3, NE, NA, NO, NO).astype(jnp.float32)
        left_half = jnp.einsum('aij,seajk->seaik', matrix, gathered)
        left_half = lax.optimization_barrier(left_half.astype(jnp.bfloat16)).astype(jnp.float32)
        sandwich = jnp.einsum('seaik,alk->seail', left_half, matrix).reshape(3, NE, NA, NO * NO)
        collected = collected + sandwich[:2] * active[None, None, :, None]
        bubble = lax.optimization_barrier(sandwich[2].astype(jnp.bfloat16)).astype(jnp.float32)
        phonon_terms = []
        for frequency in range(NW):
            start_row = (REACH + offsets[frequency]).astype(jnp.int32)
            shifted = lax.dynamic_slice_in_dim(padded_less, start_row, NE, 0).astype(jnp.float32)
            phonon_terms.append(lax.optimization_barrier(jnp.sum(bubble * shifted, axis=(0, 2))))
        return (collected, jnp.stack(phonon_terms) * (active * scale_phonon)[None, :])
    initial = jnp.zeros((2, NE, NA, NO * NO), jnp.float32)
    collected, terms = lax.scan(slot_step, initial, jnp.arange(NB, dtype=jnp.int32))
    self_energy = collected.astype(jnp.bfloat16)
    phonon_self = jnp.transpose(terms, (2, 0, 1)).reshape(NA, NB * NW)
    sigma = lax.optimization_barrier(self_energy).astype(jnp.float32).reshape(2, NE, NA, NO, NO)
    green_blocks = greens.astype(jnp.float32).reshape(2, NE, NA, NO, NO)
    gain = jnp.einsum('eaij,eajk->eik', sigma[1], green_blocks[0])
    loss = jnp.einsum('eaij,eajk->eik', sigma[0], green_blocks[1])
    current = (gain - loss).reshape(NE, NO * NO) / math.sqrt(NO * NA)
    return (self_energy, phonon_self, current)
```

```python
import math

import jax
import jax.numpy as jnp
from jax import lax
from jax.experimental import pallas as pl
from jax.experimental.pallas import tpu as pltpu
from jax.sharding import Mesh
from jax.sharding import PartitionSpec as P

NO = 16
NB = 8
NW = 16
REACH = 8
CELLS = NO * NO
BF16 = jnp.bfloat16
F32 = jnp.float32
GRID = ("x", "z", "h", "atom")

VMEM = pl.BlockSpec(memory_space=pltpu.VMEM)
SMEM = pl.BlockSpec(memory_space=pltpu.SMEM)
PARAMS = pltpu.CompilerParams(vmem_limit_bytes=12 * 1024 * 1024)


def iota(shape, axis):
    return lax.broadcasted_iota(jnp.int32, shape, axis)


def window_kernel(greens, out):
    windows = out.shape[0] // 2
    blank = jnp.zeros((8, CELLS), BF16)
    for h in range(2):
        for w in range(windows):
            for field in range(2):
                begin, end = w * 16 - 8, w * 16 + 24
                d = h * windows + w
                if w == 0:
                    out[d, field, 0:8] = blank
                    out[d, field, 8:32] = greens[field, 0, 0:end]
                elif w == windows - 1:
                    out[d, field, 0:24] = greens[field, 0, begin : end - 8]
                    out[d, field, 24:32] = blank
                else:
                    out[d, field] = greens[field, 0, begin:end]


def spread_kernel(neighbours, coupling, spread, tiled, index):
    row, col = iota((CELLS, CELLS), 0), iota((CELLS, CELLS), 1)
    pick_spread = (row // NO == col // NO).astype(F32).astype(BF16)
    pick_tiled = (row // NO == col % NO).astype(F32).astype(BF16)
    keep = iota((NO, CELLS), 0) == iota((NO, CELLS), 1) % NO
    shift = 8 - lax.axis_index("atom") * 16
    for a in range(coupling.shape[0]):
        for n in range(NB):
            index[a * NB + n] = neighbours[a, n] + shift

    def atom(a, carry):
        block = coupling[a].astype(F32)
        lines = [jnp.where(keep, block[n : n + 1], 0.0) for n in range(NB)]
        lines = jnp.concatenate(lines, axis=0).astype(BF16)
        first = jnp.dot(lines, pick_spread, preferred_element_type=F32)
        second = jnp.dot(lines, pick_tiled, preferred_element_type=F32)
        spread[a] = first.astype(BF16).reshape(NB, NO, CELLS)
        tiled[a] = second.astype(BF16).reshape(NB, NO, CELLS)
        return carry

    lax.fori_loop(0, coupling.shape[0], atom, 0)


def kron_rows(spread, tiled):
    product = spread.astype(F32)[:, None, :] * tiled.astype(F32)[None, :, :]
    return product.reshape(CELLS, CELLS).astype(BF16)


def bubble_kernel(index, spread, tiled, tile, out):
    first = lax.axis_index("h") * 8

    def atom(a, carry):
        for n in range(NB):
            matrix = kron_rows(spread[first + a, n], tiled[first + a, n])
            block = tile[1, index[(first + a) * NB + n]]
            product = jnp.dot(block, matrix, preferred_element_type=F32)
            out[a, n * 16 : n * 16 + 16] = product.astype(BF16)
        return carry

    lax.fori_loop(0, 8, atom, 0)


def overlap_kernel(bubble, tile, upper, out, frame, terms):
    first = lax.axis_index("h") * 8 + 8
    frame[...] = jnp.zeros_like(frame)
    distance = iota((32, NB * 16), 0) - iota((32, NB * 16), 1) % 16
    for a in range(8):
        frame[a, 0:16] = tile[0, first + a]
        frame[a, 16:24] = upper[a]
        overlap = lax.dot_general(
            frame[a], bubble[a], (((1,), (1,)), ((), ())), preferred_element_type=F32
        )
        parts = []
        for d in range(1, REACH + 1):
            parts.append(jnp.sum(jnp.where(distance == d, overlap, 0.0), axis=0, keepdims=True))
        terms[a] = jnp.concatenate(parts, axis=0)
    column = iota((NB * 16, NB * REACH), 1)
    gather = (iota((NB * 16, NB * REACH), 0) // 16 == column // REACH).astype(F32)
    sums = jnp.dot(
        terms[...].reshape(8 * REACH, NB * 16),
        gather,
        preferred_element_type=F32,
        precision=lax.Precision.HIGHEST,
    ).reshape(8, REACH, NB * REACH)
    same = iota((REACH, NB * REACH), 0) == iota((REACH, NB * REACH), 1) % REACH
    total = jnp.sum(jnp.where(same[None], sums, 0.0), axis=1)
    total = jnp.concatenate([total[0:4], total[4:8]], axis=1)
    for copy in range(out.shape[0]):
        out[copy] = total


def combine_kernel(parts, current, out):
    half = lax.axis_index("h")
    total = parts[0]
    for column in range(1, parts.shape[0]):
        total = total + parts[column]
    owners = current.shape[0]
    for h in range(2):
        mine = (half == h).astype(F32)
        for a in range(owners):
            d = h * owners + a
            out[d, 0:1] = current[a : a + 1, 0:128] * mine
            out[d, 1:2] = current[a : a + 1, 128:256] * mine
            out[d, 2:6] = total
            out[d, 6:8] = jnp.zeros((2, 128), F32)


def final_kernel(scale_phonon, scale_current, counts, offsets, received, phonon, current):
    atom = lax.axis_index("atom")
    owners = received.shape[0] // 2
    total = received[0]
    for source in range(1, received.shape[0]):
        total = total + received[source]
    current[0:1, 0:128] = total[0:1] * scale_current
    current[0:1, 128:256] = total[1:2] * scale_current
    sums = jnp.concatenate([received[atom, 2:6], received[owners + atom, 2:6]], axis=0)
    row, col = iota((128, 128), 0), iota((128, 128), 1)
    wanted = jnp.zeros((128, 128), jnp.int32)
    for w in range(NW):
        wanted = jnp.where(col % NW == w, offsets[w], wanted)
    slot = (row % 64) // REACH == col // NW
    match = slot & (row % REACH + 1 == wanted)
    pieces = []
    for side in range(2):
        expand = (match & (row // 64 == side)).astype(F32)
        pieces.append(
            jnp.dot(sums, expand, preferred_element_type=F32, precision=lax.Precision.HIGHEST)
        )
    values = jnp.concatenate([pieces[0][0:4], pieces[1][0:4], pieces[0][4:8], pieces[1][4:8]], axis=0)
    live = jnp.zeros((16, NB * NW), jnp.int32)
    line = iota((16, NB * NW), 0)
    for a in range(16):
        live = jnp.where(line == a, counts[a], live)
    phonon[...] = jnp.where(iota((16, NB * NW), 1) // NW < live, values * scale_phonon, 0.0)


def mix_table(phonon_weights, offsets, half):
    row, col = iota((16, 48), 0), iota((16, 48), 1)
    row_field, row_energy = row // 8, row % 8 + 8 * half
    inside = col < 32
    col_field = jnp.where(inside, col // 16, (col - 32) // 8)
    outer = jnp.where(half == 0, -8, 16)
    col_energy = jnp.where(inside, col % 16, col % 8 + outer)
    step = col_energy - row_energy
    step = jnp.where(row_field == 0, step, -step)
    table = jnp.zeros((16, 48), F32)
    for w in range(NW):
        table = table + jnp.where(step == offsets[w], phonon_weights[0, w], 0.0)
        table = table + jnp.where(step == -offsets[w], phonon_weights[1, w], 0.0)
    return jnp.where(row_field == col_field, table, 0.0).astype(BF16)


def energy_kernel(index, counts, offsets, weights, spread, tiled, tile, ring, out, mixed):
    table = mix_table(weights, offsets, lax.axis_index("h"))
    for a in range(mixed.shape[0]):
        frame = jnp.concatenate([tile[0, a], tile[1, a], ring[a]], axis=0)
        mixed[a] = jnp.dot(table, frame, preferred_element_type=F32).astype(BF16)

    def atom(a, carry):
        total = jnp.zeros((NO, CELLS), F32)
        for n in range(NB):
            matrix = kron_rows(spread[a, n], tiled[a, n])
            block = mixed[index[a * NB + n]]
            live = (n < counts[a]).astype(F32)
            total = total + live * jnp.dot(block, matrix, preferred_element_type=F32)
        out[a] = total.astype(BF16)
        return carry

    lax.fori_loop(0, out.shape[0], atom, 0)


def links(nx, nz, na, target):
    pairs = []
    for column in range(nx * nz):
        for h in range(2):
            for a in range(na):
                to, h_to, a_to = target(column, h, a)
                if 0 <= to < nx * nz and 0 <= a_to < na:
                    pairs.append(((column * 2 + h) * na + a, (to * 2 + h_to) * na + a_to))
    return pairs


def collision(sigma, green):
    sigma_blocks = sigma.reshape(2, 8, 16, NO, NO)
    green_blocks = green.reshape(2, 8, 16, NO, NO)
    gain = jnp.einsum(
        "eaij,eajk->eik", sigma_blocks[1], green_blocks[0], preferred_element_type=F32
    )
    loss = jnp.einsum(
        "eaij,eajk->eik", sigma_blocks[0], green_blocks[1], preferred_element_type=F32
    )
    return (gain - loss).reshape(8, CELLS)


def cost(flops, size):
    return pl.CostEstimate(flops=flops, bytes_accessed=size, transcendentals=0)


def shards(nx, nz, na, greens, coupling, neighbours, counts, phonon_weights, offsets):
    half = lax.axis_index("h")
    scale_phonon = 1.0 / math.sqrt(CELLS * nx * nz * 16)
    scale_current = 1.0 / math.sqrt(NO * na * 16)

    windows = pl.pallas_call(
        window_kernel,
        out_shape=jax.ShapeDtypeStruct((2 * na, 2, 32, CELLS), BF16),
        in_specs=[VMEM],
        out_specs=VMEM,
        compiler_params=PARAMS,
        cost_estimate=cost(1000, 700_000),
    )(greens)
    received = lax.all_to_all(windows, ("h", "atom"), split_axis=0, concat_axis=0, tiled=True)
    table_shape = jax.ShapeDtypeStruct((16, NB, NO, CELLS), BF16)
    spread, tiled, index = pl.pallas_call(
        spread_kernel,
        out_shape=(table_shape, table_shape, jax.ShapeDtypeStruct((16 * NB,), jnp.int32)),
        in_specs=[SMEM, VMEM],
        out_specs=(VMEM, VMEM, SMEM),
        compiler_params=PARAMS,
        cost_estimate=cost(500_000_000, 3_000_000),
    )(neighbours, coupling)

    tile = jnp.transpose(received, (1, 2, 0, 3))
    tile, spread, tiled, index = lax.optimization_barrier((tile, spread, tiled, index))
    above = lax.dynamic_slice_in_dim(tile[0, :, 0:8], 8 * half + 8, 8, 0)
    upper = lax.ppermute(above, GRID, links(nx, nz, na, lambda c, h, a: (c - 1, h, a)))
    edge = lax.dynamic_slice_in_dim(tile, 8 * (1 - half), 8, 2)
    edge = jnp.swapaxes(edge, 0, 1).reshape(32, 16, CELLS)
    ring = lax.ppermute(edge, GRID, links(nx, nz, na, lambda c, h, a: (c + 1 - 2 * h, h, a)))

    bubble = pl.pallas_call(
        bubble_kernel,
        out_shape=jax.ShapeDtypeStruct((8, NB * 16, CELLS), BF16),
        in_specs=[SMEM] + [VMEM] * 3,
        out_specs=VMEM,
        compiler_params=PARAMS,
        cost_estimate=cost(400_000_000, 4_000_000),
        name="bubble",
    )(index, spread, tiled, tile)
    phonon_part = pl.pallas_call(
        overlap_kernel,
        out_shape=jax.ShapeDtypeStruct((nx * nz, 4, 128), F32),
        in_specs=[VMEM] * 3,
        out_specs=VMEM,
        scratch_shapes=[pltpu.VMEM((8, 32, CELLS), BF16), pltpu.VMEM((8, REACH, NB * 16), F32)],
        compiler_params=PARAMS,
        cost_estimate=cost(40_000_000, 1_000_000),
        name="overlap",
    )(bubble, tile, upper)
    parts = lax.all_to_all(phonon_part, ("x", "z"), split_axis=0, concat_axis=0, tiled=True)

    ring_later, tile_later, _ = lax.optimization_barrier((ring, tile, phonon_part))
    own = jnp.swapaxes(lax.dynamic_slice_in_dim(tile_later[:, 8:24], 8 * half, 8, 2), 1, 2)
    sigma = pl.pallas_call(
        energy_kernel,
        out_shape=jax.ShapeDtypeStruct((16, 16, CELLS), BF16),
        in_specs=[SMEM] * 4 + [VMEM] * 4,
        out_specs=VMEM,
        scratch_shapes=[pltpu.VMEM((32, 16, CELLS), BF16)],
        cost_estimate=cost(800_000_000, 4_000_000),
        compiler_params=PARAMS,
        name="energy",
    )(index, counts, offsets, phonon_weights, spread, tiled, tile_later, ring_later)
    self_energy = jnp.transpose(sigma, (1, 0, 2)).reshape(2, 8, 16, CELLS)
    current_part = collision(self_energy, own)
    message = pl.pallas_call(
        combine_kernel,
        out_shape=jax.ShapeDtypeStruct((2 * na, 8, 128), F32),
        in_specs=[VMEM, VMEM],
        out_specs=VMEM,
        compiler_params=PARAMS,
        name="combine",
    )(parts, current_part)
    received_sums = lax.all_to_all(message, ("h", "atom"), split_axis=0, concat_axis=0, tiled=True)
    phonon_self, current = pl.pallas_call(
        lambda *refs: final_kernel(scale_phonon, scale_current, *refs),
        out_shape=(
            jax.ShapeDtypeStruct((16, NB * NW), F32),
            jax.ShapeDtypeStruct((1, CELLS), F32),
        ),
        in_specs=[SMEM, SMEM, VMEM],
        out_specs=(VMEM, VMEM),
        compiler_params=PARAMS,
        name="final",
    )(counts, offsets, received_sums)
    return (self_energy, phonon_self, current)


def solution(mesh):
    na = mesh.shape["atom"]
    nz = 12
    nx = mesh.shape["energy"] // (2 * nz)
    grid = Mesh(mesh.devices.reshape(nx, nz, 2, na), GRID)
    placed = (
        P(None, GRID, None, None),
        P("atom", None, None),
        P("atom", None),
        P("atom"),
        P(),
        P(),
    )

    def body(*args):
        return shards(nx, nz, na, *args)

    return jax.shard_map(
        body,
        mesh=grid,
        in_specs=placed,
        out_specs=(P(None, ("x", "z", "h"), "atom", None), P("atom", None), P(GRID, None)),
        check_vma=False,
    )
```

```python
import math

import jax
import jax.numpy as jnp
from jax import lax
from jax.experimental import pallas as pl
from jax.experimental.pallas import tpu as pltpu
from jax.sharding import Mesh
from jax.sharding import PartitionSpec as P


NO = 16
NB = 8
NW = 16
REACH = 8
CELLS = NO * NO
BF16 = jnp.bfloat16
F32 = jnp.float32
GRID = ("x", "z", "h", "atom")

VMEM = pl.BlockSpec(memory_space=pltpu.VMEM)
SMEM = pl.BlockSpec(memory_space=pltpu.SMEM)
PARAMS = pltpu.CompilerParams(vmem_limit_bytes=12 * 1024 * 1024)


def iota(shape, axis):
    return lax.broadcasted_iota(jnp.int32, shape, axis)


def window_kernel(greens, out):
    windows = out.shape[0] // 2
    blank = jnp.zeros((8, CELLS), BF16)
    for h in range(2):
        for w in range(windows):
            for field in range(2):
                begin, end = w * 16 - 8, w * 16 + 24
                d = h * windows + w
                if w == 0:
                    out[d, field, 0:8] = blank
                    out[d, field, 8:32] = greens[field, 0, 0:end]
                elif w == windows - 1:
                    out[d, field, 0:24] = greens[field, 0, begin : end - 8]
                    out[d, field, 24:32] = blank
                else:
                    out[d, field] = greens[field, 0, begin:end]


def spread_kernel(neighbours, coupling, spread, tiled, index):
    row, col = iota((CELLS, CELLS), 0), iota((CELLS, CELLS), 1)
    pick_spread = (row // NO == col // NO).astype(F32).astype(BF16)
    pick_tiled = (row // NO == col % NO).astype(F32).astype(BF16)[:, 0:128]
    keep = iota((NO, CELLS), 0) == iota((NO, CELLS), 1) % NO
    shift = 8 - lax.axis_index("atom") * 16
    for a in range(coupling.shape[0]):
        for n in range(NB):
            index[a * NB + n] = neighbours[a, n] + shift

    def atom(a, carry):
        block = coupling[a].astype(F32)
        lines = [jnp.where(keep, block[n : n + 1], 0.0) for n in range(NB)]
        lines = jnp.concatenate(lines, axis=0).astype(BF16)
        first = jnp.dot(lines, pick_spread, preferred_element_type=F32)
        second = jnp.dot(lines, pick_tiled, preferred_element_type=F32)
        spread[a] = first.astype(BF16).reshape(NB, NO, CELLS)
        tiled[a] = second.astype(BF16).reshape(NB, NO, 128)
        return carry

    lax.fori_loop(0, coupling.shape[0], atom, 0)


def kron_rows(spread, tiled):
    tiled = jnp.concatenate([tiled, tiled], axis=1)
    product = spread.astype(F32)[:, None, :] * tiled.astype(F32)[None, :, :]
    return product.reshape(CELLS, CELLS).astype(BF16)


def bubble_kernel(index, spread, tiled, tile, out, edge):
    half = lax.axis_index("h")
    first = half * 8

    def atom(a, carry):
        for n in range(NB):
            matrix = kron_rows(spread[first + a, n], tiled[first + a, n])
            block = tile[1, index[(first + a) * NB + n]]
            product = jnp.dot(block, matrix, preferred_element_type=F32)
            out[a, n * 16 : n * 16 + 16] = product.astype(BF16)
        return carry

    lax.fori_loop(0, 8, atom, 0)
    for b in range(tile.shape[1]):
        for field in range(2):
            kept = jnp.where(half == 0, tile[field, b, 8:16], tile[field, b, 0:8])
            edge[b, field * 8 : field * 8 + 8] = kept


def overlap_kernel(bubble, tile, upper, out, frame, terms):
    first = lax.axis_index("h") * 8 + 8
    frame[...] = jnp.zeros_like(frame)
    distance = iota((32, NB * 16), 0) - iota((32, NB * 16), 1) % 16
    for a in range(8):
        frame[a, 0:16] = tile[0, first + a]
        frame[a, 16:24] = upper[a]
        overlap = lax.dot_general(
            frame[a], bubble[a], (((1,), (1,)), ((), ())), preferred_element_type=F32
        )
        parts = []
        for d in range(1, REACH + 1):
            parts.append(jnp.sum(jnp.where(distance == d, overlap, 0.0), axis=0, keepdims=True))
        terms[a] = jnp.concatenate(parts, axis=0)
    column = iota((NB * 16, NB * REACH), 1)
    gather = (iota((NB * 16, NB * REACH), 0) // 16 == column // REACH).astype(F32)
    sums = jnp.dot(
        terms[...].reshape(8 * REACH, NB * 16),
        gather,
        preferred_element_type=F32,
        precision=lax.Precision.HIGHEST,
    ).reshape(8, REACH, NB * REACH)
    same = iota((REACH, NB * REACH), 0) == iota((REACH, NB * REACH), 1) % REACH
    total = jnp.sum(jnp.where(same[None], sums, 0.0), axis=1)
    total = jnp.concatenate([total[0:4], total[4:8]], axis=1)
    for copy in range(out.shape[0]):
        out[copy] = total


def combine_kernel(parts, current, out):
    half = lax.axis_index("h")
    total = parts[0]
    for column in range(1, parts.shape[0]):
        total = total + parts[column]
    owners = current.shape[0]
    for h in range(2):
        mine = (half == h).astype(F32)
        for a in range(owners):
            d = h * owners + a
            out[d, 0:1] = current[a : a + 1, 0:128] * mine
            out[d, 1:2] = current[a : a + 1, 128:256] * mine
            out[d, 2:6] = total
            out[d, 6:8] = jnp.zeros((2, 128), F32)


def final_kernel(scale_phonon, scale_current, counts, offsets, received, phonon, current):
    atom = lax.axis_index("atom")
    owners = received.shape[0] // 2
    total = received[0]
    for source in range(1, received.shape[0]):
        total = total + received[source]
    current[0:1, 0:128] = total[0:1] * scale_current
    current[0:1, 128:256] = total[1:2] * scale_current
    sums = jnp.concatenate([received[atom, 2:6], received[owners + atom, 2:6]], axis=0)
    row, col = iota((128, 128), 0), iota((128, 128), 1)
    wanted = jnp.zeros((128, 128), jnp.int32)
    for w in range(NW):
        wanted = jnp.where(col % NW == w, offsets[w], wanted)
    slot = (row % 64) // REACH == col // NW
    match = slot & (row % REACH + 1 == wanted)
    pieces = []
    for side in range(2):
        expand = (match & (row // 64 == side)).astype(F32)
        pieces.append(
            jnp.dot(sums, expand, preferred_element_type=F32, precision=lax.Precision.HIGHEST)
        )
    values = jnp.concatenate([pieces[0][0:4], pieces[1][0:4], pieces[0][4:8], pieces[1][4:8]], axis=0)
    live = jnp.zeros((16, NB * NW), jnp.int32)
    line = iota((16, NB * NW), 0)
    for a in range(16):
        live = jnp.where(line == a, counts[a], live)
    phonon[...] = jnp.where(iota((16, NB * NW), 1) // NW < live, values * scale_phonon, 0.0)


def mix_table(phonon_weights, offsets, half):
    row, col = iota((16, 48), 0), iota((16, 48), 1)
    row_field, row_energy = row // 8, row % 8 + 8 * half
    inside = col < 32
    col_field = jnp.where(inside, col // 16, (col - 32) // 8)
    outer = jnp.where(half == 0, -8, 16)
    col_energy = jnp.where(inside, col % 16, col % 8 + outer)
    step = col_energy - row_energy
    step = jnp.where(row_field == 0, step, -step)
    table = jnp.zeros((16, 48), F32)
    for w in range(NW):
        table = table + jnp.where(step == offsets[w], phonon_weights[0, w], 0.0)
        table = table + jnp.where(step == -offsets[w], phonon_weights[1, w], 0.0)
    return jnp.where(row_field == col_field, table, 0.0).astype(BF16)


def energy_kernel(index, counts, offsets, weights, spread, tiled, tile, ring, out, mixed):
    table = mix_table(weights, offsets, lax.axis_index("h"))
    for a in range(mixed.shape[0]):
        frame = jnp.concatenate([tile[0, a], tile[1, a], ring[a]], axis=0)
        mixed[a] = jnp.dot(table, frame, preferred_element_type=F32).astype(BF16)

    def atom(a, carry):
        total = jnp.zeros((NO, CELLS), F32)
        for n in range(NB):
            matrix = kron_rows(spread[a, n], tiled[a, n])
            block = mixed[index[a * NB + n]]
            live = (n < counts[a]).astype(F32)
            total = total + live * jnp.dot(block, matrix, preferred_element_type=F32)
        out[a] = total.astype(BF16)
        return carry

    lax.fori_loop(0, out.shape[0], atom, 0)


def links(nx, nz, na, target):
    pairs = []
    for column in range(nx * nz):
        for h in range(2):
            for a in range(na):
                to, h_to, a_to = target(column, h, a)
                if 0 <= to < nx * nz and 0 <= a_to < na:
                    pairs.append(((column * 2 + h) * na + a, (to * 2 + h_to) * na + a_to))
    return pairs


def collision(sigma, green):
    sigma_blocks = sigma.reshape(2, 8, 16, NO, NO)
    green_blocks = green.reshape(2, 8, 16, NO, NO)
    gain = jnp.einsum(
        "eaij,eajk->eik", sigma_blocks[1], green_blocks[0], preferred_element_type=F32
    )
    loss = jnp.einsum(
        "eaij,eajk->eik", sigma_blocks[0], green_blocks[1], preferred_element_type=F32
    )
    return (gain - loss).reshape(8, CELLS)


def cost(flops, size):
    return pl.CostEstimate(flops=flops, bytes_accessed=size, transcendentals=0)


def sandwich(index, spread, tiled, tile):
    return pl.pallas_call(
        bubble_kernel,
        out_shape=(
            jax.ShapeDtypeStruct((8, NB * 16, CELLS), BF16),
            jax.ShapeDtypeStruct((32, 16, CELLS), BF16),
        ),
        in_specs=[SMEM] + [VMEM] * 3,
        out_specs=(VMEM, VMEM),
        compiler_params=PARAMS,
        cost_estimate=cost(400_000_000, 4_000_000),
        name="bubble",
    )(index, spread, tiled, tile)


def shards(nx, nz, na, greens, coupling, neighbours, counts, phonon_weights, offsets):
    half = lax.axis_index("h")
    scale_phonon = 1.0 / math.sqrt(CELLS * nx * nz * 16)
    scale_current = 1.0 / math.sqrt(NO * na * 16)

    windows = pl.pallas_call(
        window_kernel,
        out_shape=jax.ShapeDtypeStruct((2 * na, 2, 32, CELLS), BF16),
        in_specs=[VMEM],
        out_specs=VMEM,
        compiler_params=PARAMS,
        cost_estimate=cost(1000, 700_000),
    )(greens)
    received = lax.all_to_all(windows, ("h", "atom"), split_axis=0, concat_axis=0, tiled=True)
    spread, tiled, index = pl.pallas_call(
        spread_kernel,
        out_shape=(
            jax.ShapeDtypeStruct((16, NB, NO, CELLS), BF16),
            jax.ShapeDtypeStruct((16, NB, NO, 128), BF16),
            jax.ShapeDtypeStruct((16 * NB,), jnp.int32),
        ),
        in_specs=[SMEM, VMEM],
        out_specs=(VMEM, VMEM, SMEM),
        compiler_params=PARAMS,
        cost_estimate=cost(500_000_000, 3_000_000),
    )(neighbours, coupling)

    tile = jnp.transpose(received, (1, 2, 0, 3))
    tile, spread, tiled, index = lax.optimization_barrier((tile, spread, tiled, index))
    above = lax.dynamic_slice_in_dim(tile[0, :, 0:8], 8 * half + 8, 8, 0)
    upper = lax.ppermute(above, GRID, links(nx, nz, na, lambda c, h, a: (c - 1, h, a)))
    bubble, edge = sandwich(index, spread, tiled, tile)
    ring = lax.ppermute(edge, GRID, links(nx, nz, na, lambda c, h, a: (c + 1 - 2 * h, h, a)))
    phonon_part = pl.pallas_call(
        overlap_kernel,
        out_shape=jax.ShapeDtypeStruct((nx * nz, 4, 128), F32),
        in_specs=[VMEM] * 3,
        out_specs=VMEM,
        scratch_shapes=[pltpu.VMEM((8, 32, CELLS), BF16), pltpu.VMEM((8, REACH, NB * 16), F32)],
        compiler_params=PARAMS,
        cost_estimate=cost(40_000_000, 1_000_000),
        name="overlap",
    )(bubble, tile, upper)
    parts = lax.all_to_all(phonon_part, ("x", "z"), split_axis=0, concat_axis=0, tiled=True)

    ring_later, tile_later, _ = lax.optimization_barrier((ring, tile, phonon_part))
    own = jnp.swapaxes(lax.dynamic_slice_in_dim(tile_later[:, 8:24], 8 * half, 8, 2), 1, 2)
    sigma = pl.pallas_call(
        energy_kernel,
        out_shape=jax.ShapeDtypeStruct((16, 16, CELLS), BF16),
        in_specs=[SMEM] * 4 + [VMEM] * 4,
        out_specs=VMEM,
        scratch_shapes=[pltpu.VMEM((32, 16, CELLS), BF16)],
        cost_estimate=cost(800_000_000, 4_000_000),
        compiler_params=PARAMS,
        name="energy",
    )(index, counts, offsets, phonon_weights, spread, tiled, tile_later, ring_later)
    self_energy = jnp.transpose(sigma, (1, 0, 2)).reshape(2, 8, 16, CELLS)
    current_part = collision(self_energy, own)
    message = pl.pallas_call(
        combine_kernel,
        out_shape=jax.ShapeDtypeStruct((2 * na, 8, 128), F32),
        in_specs=[VMEM, VMEM],
        out_specs=VMEM,
        compiler_params=PARAMS,
        name="combine",
    )(parts, current_part)
    received_sums = lax.all_to_all(message, ("h", "atom"), split_axis=0, concat_axis=0, tiled=True)
    phonon_self, current = pl.pallas_call(
        lambda *refs: final_kernel(scale_phonon, scale_current, *refs),
        out_shape=(
            jax.ShapeDtypeStruct((16, NB * NW), F32),
            jax.ShapeDtypeStruct((1, CELLS), F32),
        ),
        in_specs=[SMEM, SMEM, VMEM],
        out_specs=(VMEM, VMEM),
        compiler_params=PARAMS,
        name="final",
    )(counts, offsets, received_sums)
    return (self_energy, phonon_self, current)


def solution(mesh):
    na = mesh.shape["atom"]
    nz = 12
    nx = mesh.shape["energy"] // (2 * nz)
    grid = Mesh(mesh.devices.reshape(nx, nz, 2, na), GRID)
    placed = (
        P(None, GRID, None, None),
        P("atom", None, None),
        P("atom", None),
        P("atom"),
        P(),
        P(),
    )

    def body(*args):
        return shards(nx, nz, na, *args)

    return jax.shard_map(
        body,
        mesh=grid,
        in_specs=placed,
        out_specs=(P(None, ("x", "z", "h"), "atom", None), P("atom", None), P(GRID, None)),
        check_vma=False,
    )
```

```python
import math

import jax
import jax.numpy as jnp
from jax import lax
from jax.experimental import pallas as pl
from jax.experimental.pallas import tpu as pltpu
from jax.sharding import Mesh
from jax.sharding import PartitionSpec as P


NO = 16
NB = 8
NW = 16
REACH = 8
CELLS = NO * NO
BF16 = jnp.bfloat16
F32 = jnp.float32
GRID = ("x", "z", "h", "atom")

VMEM = pl.BlockSpec(memory_space=pltpu.VMEM)
SMEM = pl.BlockSpec(memory_space=pltpu.SMEM)
PARAMS = pltpu.CompilerParams(vmem_limit_bytes=12 * 1024 * 1024)


def iota(shape, axis):
    return lax.broadcasted_iota(jnp.int32, shape, axis)


def window_kernel(greens, out):
    windows = out.shape[0] // 2
    blank = jnp.zeros((8, CELLS), BF16)
    for h in range(2):
        for w in range(windows):
            for field in range(2):
                begin, end = w * 16 - 8, w * 16 + 24
                d = h * windows + w
                if w == 0:
                    out[d, field, 0:8] = blank
                    out[d, field, 8:32] = greens[field, 0, 0:end]
                elif w == windows - 1:
                    out[d, field, 0:24] = greens[field, 0, begin : end - 8]
                    out[d, field, 24:32] = blank
                else:
                    out[d, field] = greens[field, 0, begin:end]


def prepare_kernel(scale, neighbours, counts, offsets, coupling, spread, tiled, index, picks, live):
    row, col = iota((CELLS, CELLS), 0), iota((CELLS, CELLS), 1)
    pick_spread = (row // NO == col // NO).astype(F32).astype(BF16)
    pick_tiled = (row // NO == col % NO).astype(F32).astype(BF16)[:, 0:128]
    keep = iota((NO, CELLS), 0) == iota((NO, CELLS), 1) % NO
    shift = 8 - lax.axis_index("atom") * 16
    for a in range(coupling.shape[0]):
        for n in range(NB):
            index[a * NB + n] = neighbours[a, n] + shift
    line = iota((8, 256), 1) % 128
    wanted = jnp.zeros((8, 256), jnp.int32)
    for w in range(NW):
        wanted = jnp.where(line % NW == w, offsets[w], wanted)
    source_row = iota((8, 256), 1) // 128 * 64 + line // NW * REACH + wanted - 1
    picks[...] = (iota((128, 256), 0) == source_row[0:1]).astype(F32).astype(BF16)
    used = jnp.zeros((16, NB * NW), jnp.int32)
    for a in range(16):
        used = jnp.where(iota((16, NB * NW), 0) == a, counts[a], used)
    live[...] = jnp.where(iota((16, NB * NW), 1) // NW < used, scale, 0.0)

    def atom(a, carry):
        block = coupling[a].astype(F32)
        lines = [jnp.where(keep, block[n : n + 1], 0.0) for n in range(NB)]
        lines = jnp.concatenate(lines, axis=0).astype(BF16)
        first = jnp.dot(lines, pick_spread, preferred_element_type=F32)
        second = jnp.dot(lines, pick_tiled, preferred_element_type=F32)
        spread[a] = first.astype(BF16).reshape(NB, NO, CELLS)
        tiled[a] = second.astype(BF16).reshape(NB, NO, 128)
        return carry

    lax.fori_loop(0, coupling.shape[0], atom, 0)


def exact_select(values, picks):
    high = values.astype(BF16)
    rest = values - high.astype(F32)
    middle = rest.astype(BF16)
    low = (rest - middle.astype(F32)).astype(BF16)
    count = values.shape[0]
    stacked = jnp.concatenate([high, middle, low], axis=0)
    chosen = jnp.dot(stacked, picks, preferred_element_type=F32)
    return chosen[0:count] + (chosen[count : 2 * count] + chosen[2 * count : 3 * count])


def kron_rows(spread, tiled):
    tiled = jnp.concatenate([tiled, tiled], axis=1)
    product = spread.astype(F32)[:, None, :] * tiled.astype(F32)[None, :, :]
    return product.reshape(CELLS, CELLS).astype(BF16)


def bubble_kernel(index_at, spread, tiled, tile, out, edge, index, arrived):
    half = lax.axis_index("h")
    first = half * 8
    load = pltpu.make_async_copy(index_at, index, arrived)
    load.start()
    for b in range(tile.shape[1]):
        for field in range(2):
            kept = jnp.where(half == 0, tile[field, b, 8:16], tile[field, b, 0:8])
            edge[b, field * 8 : field * 8 + 8] = kept
    load.wait()

    def atom(a, carry):
        for n in range(NB):
            matrix = kron_rows(spread[first + a, n], tiled[first + a, n])
            block = tile[1, index[(first + a) * NB + n]]
            product = jnp.dot(block, matrix, preferred_element_type=F32)
            out[a, n * 16 : n * 16 + 16] = product.astype(BF16)
        return carry

    lax.fori_loop(0, 8, atom, 0)


def overlap_kernel(bubble, tile, upper, out, frame, terms):
    first = lax.axis_index("h") * 8 + 8
    frame[...] = jnp.zeros_like(frame)
    distance = iota((32, NB * 16), 0) - iota((32, NB * 16), 1) % 16
    for a in range(8):
        frame[a, 0:16] = tile[0, first + a]
        frame[a, 16:24] = upper[a]
        overlap = lax.dot_general(
            frame[a], bubble[a], (((1,), (1,)), ((), ())), preferred_element_type=F32
        )
        parts = []
        for d in range(1, REACH + 1):
            parts.append(jnp.sum(jnp.where(distance == d, overlap, 0.0), axis=0, keepdims=True))
        terms[a] = jnp.concatenate(parts, axis=0)
    column = iota((NB * 16, NB * REACH), 1)
    gather = iota((NB * 16, NB * REACH), 0) // 16 == column // REACH
    gather = gather.astype(F32).astype(BF16)
    sums = exact_select(terms[...].reshape(8 * REACH, NB * 16), gather)
    sums = sums.reshape(8, REACH, NB * REACH)
    same = iota((REACH, NB * REACH), 0) == iota((REACH, NB * REACH), 1) % REACH
    total = jnp.sum(jnp.where(same[None], sums, 0.0), axis=1)
    total = jnp.concatenate([total[0:4], total[4:8]], axis=1).astype(BF16)
    for copy in range(out.shape[0]):
        out[copy] = total


def combine_kernel(parts, current, out):
    half = lax.axis_index("h")
    total = parts[0].astype(F32)
    for column in range(1, parts.shape[0]):
        total = total + parts[column].astype(F32)
    owners = current.shape[0]
    for h in range(2):
        mine = (half == h).astype(F32)
        for a in range(owners):
            d = h * owners + a
            out[d, 0, 0:1] = current[a : a + 1, 0:128] * mine
            out[d, 0, 1:2] = current[a : a + 1, 128:256] * mine
            out[d, 1] = total[0:2]
            out[d, 2] = total[2:4]


def final_kernel(scale, received, picks, live, phonon, current):
    atom = lax.axis_index("atom")
    other = received.shape[0] // 2 + atom
    total = received[0, 0]
    for source in range(1, received.shape[0]):
        total = total + received[source, 0]
    current[0:1, 0:128] = total[0:1] * scale
    current[0:1, 128:256] = total[1:2] * scale
    sums = jnp.concatenate(
        [received[atom, 1], received[atom, 2], received[other, 1], received[other, 2]], axis=0
    )
    values = exact_select(sums, picks[...])
    near, far = values[:, 0:128], values[:, 128:256]
    values = jnp.concatenate([near[0:4], far[0:4], near[4:8], far[4:8]], axis=0)
    phonon[...] = values * live[...]


def mix_table(phonon_weights, offsets, half):
    row, col = iota((16, 48), 0), iota((16, 48), 1)
    row_field, row_energy = row // 8, row % 8 + 8 * half
    inside = col < 32
    col_field = jnp.where(inside, col // 16, (col - 32) // 8)
    outer = jnp.where(half == 0, -8, 16)
    col_energy = jnp.where(inside, col % 16, col % 8 + outer)
    step = col_energy - row_energy
    step = jnp.where(row_field == 0, step, -step)
    table = jnp.zeros((16, 48), F32)
    for w in range(NW):
        table = table + jnp.where(step == offsets[w], phonon_weights[0, w], 0.0)
        table = table + jnp.where(step == -offsets[w], phonon_weights[1, w], 0.0)
    return jnp.where(row_field == col_field, table, 0.0).astype(BF16)


def energy_kernel(index, counts, offsets, weights, spread, tiled, tile, ring, out, mixed):
    table = mix_table(weights, offsets, lax.axis_index("h"))
    for a in range(mixed.shape[0]):
        frame = jnp.concatenate([tile[0, a], tile[1, a], ring[a]], axis=0)
        mixed[a] = jnp.dot(table, frame, preferred_element_type=F32).astype(BF16)

    def atom(a, carry):
        total = jnp.zeros((NO, CELLS), F32)
        for n in range(NB):
            matrix = kron_rows(spread[a, n], tiled[a, n])
            block = mixed[index[a * NB + n]]
            live = (n < counts[a]).astype(F32)
            total = total + live * jnp.dot(block, matrix, preferred_element_type=F32)
        out[a] = total.astype(BF16)
        return carry

    lax.fori_loop(0, out.shape[0], atom, 0)


def links(nx, nz, na, target):
    pairs = []
    for column in range(nx * nz):
        for h in range(2):
            for a in range(na):
                to, h_to, a_to = target(column, h, a)
                if 0 <= to < nx * nz and 0 <= a_to < na:
                    pairs.append(((column * 2 + h) * na + a, (to * 2 + h_to) * na + a_to))
    return pairs


def collision(sigma, green):
    sigma_blocks = sigma.reshape(2, 8, 16, NO, NO)
    green_blocks = green.reshape(2, 8, 16, NO, NO)
    gain = jnp.einsum(
        "eaij,eajk->eik", sigma_blocks[1], green_blocks[0], preferred_element_type=F32
    )
    loss = jnp.einsum(
        "eaij,eajk->eik", sigma_blocks[0], green_blocks[1], preferred_element_type=F32
    )
    return (gain - loss).reshape(8, CELLS)


def cost(flops, size):
    return pl.CostEstimate(flops=flops, bytes_accessed=size, transcendentals=0)


def sandwich(index, spread, tiled, tile):
    return pl.pallas_call(
        bubble_kernel,
        out_shape=(
            jax.ShapeDtypeStruct((8, NB * 16, CELLS), BF16),
            jax.ShapeDtypeStruct((32, 16, CELLS), BF16),
        ),
        in_specs=[pl.BlockSpec(memory_space=pl.ANY)] + [VMEM] * 3,
        out_specs=(VMEM, VMEM),
        scratch_shapes=[pltpu.SMEM((16 * NB,), jnp.int32), pltpu.SemaphoreType.DMA],
        compiler_params=PARAMS,
        cost_estimate=cost(400_000_000, 4_000_000),
        name="bubble",
    )(index, spread, tiled, tile)


def shards(nx, nz, na, greens, coupling, neighbours, counts, phonon_weights, offsets):
    half = lax.axis_index("h")
    scale_phonon = 1.0 / math.sqrt(CELLS * nx * nz * 16)
    scale_current = 1.0 / math.sqrt(NO * na * 16)

    windows = pl.pallas_call(
        window_kernel,
        out_shape=jax.ShapeDtypeStruct((2 * na, 2, 32, CELLS), BF16),
        in_specs=[VMEM],
        out_specs=VMEM,
        compiler_params=PARAMS,
        cost_estimate=cost(1000, 700_000),
    )(greens)
    received = lax.all_to_all(windows, ("h", "atom"), split_axis=0, concat_axis=0, tiled=True)
    spread, tiled, index, picks, live = pl.pallas_call(
        lambda *refs: prepare_kernel(scale_phonon, *refs),
        out_shape=(
            jax.ShapeDtypeStruct((16, NB, NO, CELLS), BF16),
            jax.ShapeDtypeStruct((16, NB, NO, 128), BF16),
            jax.ShapeDtypeStruct((16 * NB,), jnp.int32),
            jax.ShapeDtypeStruct((128, 256), BF16),
            jax.ShapeDtypeStruct((16, NB * NW), F32),
        ),
        in_specs=[SMEM, SMEM, SMEM, VMEM],
        out_specs=(VMEM, VMEM, SMEM, VMEM, VMEM),
        compiler_params=PARAMS,
        cost_estimate=cost(500_000_000, 3_000_000),
    )(neighbours, counts, offsets, coupling)

    tile = jnp.transpose(received, (1, 2, 0, 3))
    tile, spread, tiled, index = lax.optimization_barrier((tile, spread, tiled, index))
    above = lax.dynamic_slice_in_dim(tile[0, :, 0:8], 8 * half + 8, 8, 0)
    upper = lax.ppermute(above, GRID, links(nx, nz, na, lambda c, h, a: (c - 1, h, a)))
    bubble, edge = sandwich(index, spread, tiled, tile)
    ring = lax.ppermute(edge, GRID, links(nx, nz, na, lambda c, h, a: (c + 1 - 2 * h, h, a)))
    phonon_part = pl.pallas_call(
        overlap_kernel,
        out_shape=jax.ShapeDtypeStruct((nx * nz, 4, 128), BF16),
        in_specs=[VMEM] * 3,
        out_specs=VMEM,
        scratch_shapes=[pltpu.VMEM((8, 32, CELLS), BF16), pltpu.VMEM((8, REACH, NB * 16), F32)],
        compiler_params=PARAMS,
        cost_estimate=cost(40_000_000, 1_000_000),
        name="overlap",
    )(bubble, tile, upper)
    parts = lax.all_to_all(phonon_part, ("x", "z"), split_axis=0, concat_axis=0, tiled=True)

    ring_later, tile_later, _ = lax.optimization_barrier((ring, tile, phonon_part))
    own = jnp.swapaxes(lax.dynamic_slice_in_dim(tile_later[:, 8:24], 8 * half, 8, 2), 1, 2)
    sigma = pl.pallas_call(
        energy_kernel,
        out_shape=jax.ShapeDtypeStruct((16, 16, CELLS), BF16),
        in_specs=[SMEM] * 4 + [VMEM] * 4,
        out_specs=VMEM,
        scratch_shapes=[pltpu.VMEM((32, 16, CELLS), BF16)],
        cost_estimate=cost(800_000_000, 4_000_000),
        compiler_params=PARAMS,
        name="energy",
    )(index, counts, offsets, phonon_weights, spread, tiled, tile_later, ring_later)
    self_energy = jnp.transpose(sigma, (1, 0, 2)).reshape(2, 8, 16, CELLS)
    current_part = collision(self_energy, own)
    message = pl.pallas_call(
        combine_kernel,
        out_shape=jax.ShapeDtypeStruct((2 * na, 3, 2, 128), F32),
        in_specs=[VMEM, VMEM],
        out_specs=VMEM,
        compiler_params=PARAMS,
        name="combine",
    )(parts, current_part)
    received_sums = lax.all_to_all(message, ("h", "atom"), split_axis=0, concat_axis=0, tiled=True)
    phonon_self, current = pl.pallas_call(
        lambda *refs: final_kernel(scale_current, *refs),
        out_shape=(
            jax.ShapeDtypeStruct((16, NB * NW), F32),
            jax.ShapeDtypeStruct((1, CELLS), F32),
        ),
        in_specs=[VMEM] * 3,
        out_specs=(VMEM, VMEM),
        compiler_params=PARAMS,
        name="final",
    )(received_sums, picks, live)
    return (self_energy, phonon_self, current)


def solution(mesh):
    na = mesh.shape["atom"]
    nz = 12
    nx = mesh.shape["energy"] // (2 * nz)
    grid = Mesh(mesh.devices.reshape(nx, nz, 2, na), GRID)
    placed = (
        P(None, GRID, None, None),
        P("atom", None, None),
        P("atom", None),
        P("atom"),
        P(),
        P(),
    )

    def body(*args):
        return shards(nx, nz, na, *args)

    return jax.shard_map(
        body,
        mesh=grid,
        in_specs=placed,
        out_specs=(P(None, ("x", "z", "h"), "atom", None), P("atom", None), P(GRID, None)),
        check_vma=False,
    )
```

```python
import math

import jax
import jax.numpy as jnp
from jax import lax
from jax.experimental import pallas as pl
from jax.experimental.pallas import tpu as pltpu
from jax.sharding import Mesh
from jax.sharding import PartitionSpec as P


NO = 16
NB = 8
NW = 16
REACH = 8
CELLS = NO * NO
BF16 = jnp.bfloat16
F32 = jnp.float32
GRID = ("x", "z", "h", "atom")

VMEM = pl.BlockSpec(memory_space=pltpu.VMEM)
SMEM = pl.BlockSpec(memory_space=pltpu.SMEM)
PARAMS = pltpu.CompilerParams(vmem_limit_bytes=12 * 1024 * 1024)


def iota(shape, axis):
    return lax.broadcasted_iota(jnp.int32, shape, axis)


def window_kernel(greens, out):
    windows = out.shape[0] // 2
    blank = jnp.zeros((8, CELLS), BF16)
    for h in range(2):
        for w in range(windows):
            for field in range(2):
                begin, end = w * 16 - 8, w * 16 + 24
                d = h * windows + w
                if w == 0:
                    out[d, field, 0:8] = blank
                    out[d, field, 8:32] = greens[field, 0, 0:end]
                elif w == windows - 1:
                    out[d, field, 0:24] = greens[field, 0, begin : end - 8]
                    out[d, field, 24:32] = blank
                else:
                    out[d, field] = greens[field, 0, begin:end]


def prepare_kernel(scale, neighbours, counts, offsets, coupling, spread, tiled, index, picks, live):
    row, col = iota((CELLS, CELLS), 0), iota((CELLS, CELLS), 1)
    pick_spread = (row // NO == col // NO).astype(F32).astype(BF16)
    pick_tiled = (row // NO == col % NO).astype(F32).astype(BF16)[:, 0:128]
    keep = iota((NO, CELLS), 0) == iota((NO, CELLS), 1) % NO
    shift = 8 - lax.axis_index("atom") * 16
    for a in range(coupling.shape[0]):
        for n in range(NB):
            index[a * NB + n] = neighbours[a, n] + shift
    line = iota((8, 256), 1) % 128
    wanted = jnp.zeros((8, 256), jnp.int32)
    for w in range(NW):
        wanted = jnp.where(line % NW == w, offsets[w], wanted)
    source_row = iota((8, 256), 1) // 128 * 64 + line // NW * REACH + wanted - 1
    picks[...] = (iota((128, 256), 0) == source_row[0:1]).astype(F32).astype(BF16)
    used = jnp.zeros((16, NB * NW), jnp.int32)
    for a in range(16):
        used = jnp.where(iota((16, NB * NW), 0) == a, counts[a], used)
    live[...] = jnp.where(iota((16, NB * NW), 1) // NW < used, scale, 0.0)

    def atom(a, carry):
        block = coupling[a].astype(F32)
        lines = [jnp.where(keep, block[n : n + 1], 0.0) for n in range(NB)]
        lines = jnp.concatenate(lines, axis=0).astype(BF16)
        first = jnp.dot(lines, pick_spread, preferred_element_type=F32)
        second = jnp.dot(lines, pick_tiled, preferred_element_type=F32)
        spread[a] = first.astype(BF16).reshape(NB, NO, CELLS)
        tiled[a] = second.astype(BF16).reshape(NB, NO, 128)
        return carry

    lax.fori_loop(0, coupling.shape[0], atom, 0)


def exact_select(values, picks):
    high = values.astype(BF16)
    rest = values - high.astype(F32)
    middle = rest.astype(BF16)
    low = (rest - middle.astype(F32)).astype(BF16)
    count = values.shape[0]
    stacked = jnp.concatenate([high, middle, low], axis=0)
    chosen = jnp.dot(stacked, picks, preferred_element_type=F32)
    return chosen[0:count] + (chosen[count : 2 * count] + chosen[2 * count : 3 * count])


def kron_rows(spread, tiled):
    tiled = jnp.concatenate([tiled, tiled], axis=1)
    product = spread.astype(F32)[:, None, :] * tiled.astype(F32)[None, :, :]
    return product.reshape(CELLS, CELLS).astype(BF16)


def bubble_kernel(index_at, spread, tiled, tile, out, edge, index, arrived):
    half = lax.axis_index("h")
    first = half * 8
    load = pltpu.make_async_copy(index_at, index, arrived)
    load.start()
    for b in range(tile.shape[1]):
        for field in range(2):
            kept = jnp.where(half == 0, tile[field, b, 8:16], tile[field, b, 0:8])
            edge[b, field * 8 : field * 8 + 8] = kept
    load.wait()

    for a in range(out.shape[0]):
        for n in range(NB):
            matrix = kron_rows(spread[first + a, n], tiled[first + a, n])
            block = tile[1, index[(first + a) * NB + n]]
            product = jnp.dot(block, matrix, preferred_element_type=F32)
            out[a, n * 16 : n * 16 + 16] = product.astype(BF16)


def overlap_kernel(bubble, tile, upper, out, frame, terms):
    first = lax.axis_index("h") * 8 + 8
    frame[...] = jnp.zeros_like(frame)
    distance = iota((32, NB * 16), 0) - iota((32, NB * 16), 1) % 16
    for a in range(8):
        frame[a, 0:16] = tile[0, first + a]
        frame[a, 16:24] = upper[a]
        overlap = lax.dot_general(
            frame[a], bubble[a], (((1,), (1,)), ((), ())), preferred_element_type=F32
        )
        parts = []
        for d in range(1, REACH + 1):
            parts.append(jnp.sum(jnp.where(distance == d, overlap, 0.0), axis=0, keepdims=True))
        terms[a] = jnp.concatenate(parts, axis=0)
    column = iota((NB * 16, NB * REACH), 1)
    gather = iota((NB * 16, NB * REACH), 0) // 16 == column // REACH
    gather = gather.astype(F32).astype(BF16)
    sums = exact_select(terms[...].reshape(8 * REACH, NB * 16), gather)
    sums = sums.reshape(8, REACH, NB * REACH)
    same = iota((REACH, NB * REACH), 0) == iota((REACH, NB * REACH), 1) % REACH
    total = jnp.sum(jnp.where(same[None], sums, 0.0), axis=1)
    total = jnp.concatenate([total[0:4], total[4:8]], axis=1).astype(BF16)
    for copy in range(out.shape[0]):
        out[copy] = total


def combine_kernel(parts, current, out):
    half = lax.axis_index("h")
    total = parts[0].astype(F32)
    for column in range(1, parts.shape[0]):
        total = total + parts[column].astype(F32)
    owners = current.shape[0]
    for h in range(2):
        mine = (half == h).astype(F32)
        for a in range(owners):
            d = h * owners + a
            out[d, 0, 0:1] = current[a : a + 1, 0:128] * mine
            out[d, 0, 1:2] = current[a : a + 1, 128:256] * mine
            out[d, 1] = total[0:2]
            out[d, 2] = total[2:4]


def final_kernel(scale, received, picks, live, phonon, current):
    atom = lax.axis_index("atom")
    other = received.shape[0] // 2 + atom
    total = received[0, 0]
    for source in range(1, received.shape[0]):
        total = total + received[source, 0]
    current[0:1, 0:128] = total[0:1] * scale
    current[0:1, 128:256] = total[1:2] * scale
    sums = jnp.concatenate(
        [received[atom, 1], received[atom, 2], received[other, 1], received[other, 2]], axis=0
    )
    values = exact_select(sums, picks[...])
    near, far = values[:, 0:128], values[:, 128:256]
    values = jnp.concatenate([near[0:4], far[0:4], near[4:8], far[4:8]], axis=0)
    phonon[...] = values * live[...]


def mix_table(phonon_weights, offsets, half):
    row, col = iota((16, 48), 0), iota((16, 48), 1)
    row_field, row_energy = row // 8, row % 8 + 8 * half
    inside = col < 32
    col_field = jnp.where(inside, col // 16, (col - 32) // 8)
    outer = jnp.where(half == 0, -8, 16)
    col_energy = jnp.where(inside, col % 16, col % 8 + outer)
    step = col_energy - row_energy
    step = jnp.where(row_field == 0, step, -step)
    table = jnp.zeros((16, 48), F32)
    for w in range(NW):
        table = table + jnp.where(step == offsets[w], phonon_weights[0, w], 0.0)
        table = table + jnp.where(step == -offsets[w], phonon_weights[1, w], 0.0)
    return jnp.where(row_field == col_field, table, 0.0).astype(BF16)


def energy_kernel(index, counts, offsets, weights, spread, tiled, tile, ring, out, mixed):
    table = mix_table(weights, offsets, lax.axis_index("h"))
    for a in range(mixed.shape[0]):
        frame = jnp.concatenate([tile[0, a], tile[1, a], ring[a]], axis=0)
        mixed[a] = jnp.dot(table, frame, preferred_element_type=F32).astype(BF16)

    for a in range(out.shape[0]):
        total = jnp.zeros((NO, CELLS), F32)
        for n in range(NB):
            matrix = kron_rows(spread[a, n], tiled[a, n])
            block = mixed[index[a * NB + n]]
            live = (n < counts[a]).astype(F32)
            total = total + live * jnp.dot(block, matrix, preferred_element_type=F32)
        out[a] = total.astype(BF16)


def links(nx, nz, na, target):
    pairs = []
    for column in range(nx * nz):
        for h in range(2):
            for a in range(na):
                to, h_to, a_to = target(column, h, a)
                if 0 <= to < nx * nz and 0 <= a_to < na:
                    pairs.append(((column * 2 + h) * na + a, (to * 2 + h_to) * na + a_to))
    return pairs


def collision(sigma, green):
    sigma_blocks = sigma.reshape(2, 8, 16, NO, NO)
    green_blocks = green.reshape(2, 8, 16, NO, NO)
    gain = jnp.einsum(
        "eaij,eajk->eik", sigma_blocks[1], green_blocks[0], preferred_element_type=F32
    )
    loss = jnp.einsum(
        "eaij,eajk->eik", sigma_blocks[0], green_blocks[1], preferred_element_type=F32
    )
    return (gain - loss).reshape(8, CELLS)


def cost(flops, size):
    return pl.CostEstimate(flops=flops, bytes_accessed=size, transcendentals=0)


def sandwich(index, spread, tiled, tile):
    return pl.pallas_call(
        bubble_kernel,
        out_shape=(
            jax.ShapeDtypeStruct((8, NB * 16, CELLS), BF16),
            jax.ShapeDtypeStruct((32, 16, CELLS), BF16),
        ),
        in_specs=[pl.BlockSpec(memory_space=pl.ANY)] + [VMEM] * 3,
        out_specs=(VMEM, VMEM),
        scratch_shapes=[pltpu.SMEM((16 * NB,), jnp.int32), pltpu.SemaphoreType.DMA],
        compiler_params=PARAMS,
        cost_estimate=cost(400_000_000, 4_000_000),
        name="bubble",
    )(index, spread, tiled, tile)


def shards(nx, nz, na, greens, coupling, neighbours, counts, phonon_weights, offsets):
    half = lax.axis_index("h")
    scale_phonon = 1.0 / math.sqrt(CELLS * nx * nz * 16)
    scale_current = 1.0 / math.sqrt(NO * na * 16)

    windows = pl.pallas_call(
        window_kernel,
        out_shape=jax.ShapeDtypeStruct((2 * na, 2, 32, CELLS), BF16),
        in_specs=[VMEM],
        out_specs=VMEM,
        compiler_params=PARAMS,
        cost_estimate=cost(1000, 700_000),
    )(greens)
    received = lax.all_to_all(windows, ("h", "atom"), split_axis=0, concat_axis=0, tiled=True)
    spread, tiled, index, picks, live = pl.pallas_call(
        lambda *refs: prepare_kernel(scale_phonon, *refs),
        out_shape=(
            jax.ShapeDtypeStruct((16, NB, NO, CELLS), BF16),
            jax.ShapeDtypeStruct((16, NB, NO, 128), BF16),
            jax.ShapeDtypeStruct((16 * NB,), jnp.int32),
            jax.ShapeDtypeStruct((128, 256), BF16),
            jax.ShapeDtypeStruct((16, NB * NW), F32),
        ),
        in_specs=[SMEM, SMEM, SMEM, VMEM],
        out_specs=(VMEM, VMEM, SMEM, VMEM, VMEM),
        compiler_params=PARAMS,
        cost_estimate=cost(500_000_000, 3_000_000),
    )(neighbours, counts, offsets, coupling)

    tile = jnp.transpose(received, (1, 2, 0, 3))
    tile, spread, tiled, index = lax.optimization_barrier((tile, spread, tiled, index))
    above = lax.dynamic_slice_in_dim(tile[0, :, 0:8], 8 * half + 8, 8, 0)
    upper = lax.ppermute(above, GRID, links(nx, nz, na, lambda c, h, a: (c - 1, h, a)))
    bubble, edge = sandwich(index, spread, tiled, tile)
    ring = lax.ppermute(edge, GRID, links(nx, nz, na, lambda c, h, a: (c + 1 - 2 * h, h, a)))
    phonon_part = pl.pallas_call(
        overlap_kernel,
        out_shape=jax.ShapeDtypeStruct((nx * nz, 4, 128), BF16),
        in_specs=[VMEM] * 3,
        out_specs=VMEM,
        scratch_shapes=[pltpu.VMEM((8, 32, CELLS), BF16), pltpu.VMEM((8, REACH, NB * 16), F32)],
        compiler_params=PARAMS,
        cost_estimate=cost(40_000_000, 1_000_000),
        name="overlap",
    )(bubble, tile, upper)
    parts = lax.all_to_all(phonon_part, ("x", "z"), split_axis=0, concat_axis=0, tiled=True)

    ring_later, tile_later, _ = lax.optimization_barrier((ring, tile, phonon_part))
    own = jnp.swapaxes(lax.dynamic_slice_in_dim(tile_later[:, 8:24], 8 * half, 8, 2), 1, 2)
    sigma = pl.pallas_call(
        energy_kernel,
        out_shape=jax.ShapeDtypeStruct((16, 16, CELLS), BF16),
        in_specs=[SMEM] * 4 + [VMEM] * 4,
        out_specs=VMEM,
        scratch_shapes=[pltpu.VMEM((32, 16, CELLS), BF16)],
        cost_estimate=cost(800_000_000, 4_000_000),
        compiler_params=PARAMS,
        name="energy",
    )(index, counts, offsets, phonon_weights, spread, tiled, tile_later, ring_later)
    self_energy = jnp.transpose(sigma, (1, 0, 2)).reshape(2, 8, 16, CELLS)
    current_part = collision(self_energy, own)
    message = pl.pallas_call(
        combine_kernel,
        out_shape=jax.ShapeDtypeStruct((2 * na, 3, 2, 128), F32),
        in_specs=[VMEM, VMEM],
        out_specs=VMEM,
        compiler_params=PARAMS,
        name="combine",
    )(parts, current_part)
    received_sums = lax.all_to_all(message, ("h", "atom"), split_axis=0, concat_axis=0, tiled=True)
    phonon_self, current = pl.pallas_call(
        lambda *refs: final_kernel(scale_current, *refs),
        out_shape=(
            jax.ShapeDtypeStruct((16, NB * NW), F32),
            jax.ShapeDtypeStruct((1, CELLS), F32),
        ),
        in_specs=[VMEM] * 3,
        out_specs=(VMEM, VMEM),
        compiler_params=PARAMS,
        name="final",
    )(received_sums, picks, live)
    return (self_energy, phonon_self, current)


def solution(mesh):
    na = mesh.shape["atom"]
    nz = 12
    nx = mesh.shape["energy"] // (2 * nz)
    grid = Mesh(mesh.devices.reshape(nx, nz, 2, na), GRID)
    placed = (
        P(None, GRID, None, None),
        P("atom", None, None),
        P("atom", None),
        P("atom"),
        P(),
        P(),
    )

    def body(*args):
        return shards(nx, nz, na, *args)

    return jax.shard_map(
        body,
        mesh=grid,
        in_specs=placed,
        out_specs=(P(None, ("x", "z", "h"), "atom", None), P("atom", None), P(GRID, None)),
        check_vma=False,
    )
```
